32 devices in a mesh: row: 8 (over y, x, core), col: 4 (over z).
Axes of the slice: x: 2, y: 2, z: 4, core: 2. Of those that a mesh axis runs over, the one named last changes fastest.
Arguments:
- chol: float32 [12288, 640], P(('row', 'col')), may hold values from -6 to 6
- eps_occ: float32 [48], replicated, may hold values from -2 to -0.5
- eps_vir: float32 [256], replicated, may hold values from 0.3 to 3
Outputs:
- work: float32 [12288, 640], P(('row', 'col'))
- energies: float32 [2], replicated
The draws below stay inside these ranges and needn't reach their ends.
All inputs are finite; a program needn't handle non-finite values.
Results may differ from the reference program's by a relative error of at most 0.00013.
Values sent between devices are 32-bit elements; how exact they have to be, the bound alone decides.
A program may use at most 192 MiB of HBM per device.

```python
import jax
import jax.numpy as jnp
from jax import lax

NO = 48
NV = 256
NAUX = 640
ITERS = 2
OV = 12288


def block_scale(own_key, shape, shards, least, top_value):
    loudness = 1.0
    for position, parts in shards:
        heights = jax.random.uniform(jax.random.fold_in(jax.random.fold_in(own_key, 6), position), (parts,), jnp.float32, least / len(shards), top_value / len(shards))
        loudness = loudness * jnp.repeat(jnp.exp(heights), shape[position] // parts).reshape((-1,) + (1,) * (len(shape) - 1 - position))
    return loudness


def normal_values(own_key, extent, scale, bound, split=(), kind=jnp.bfloat16):
    entries = jax.random.normal(own_key, extent, jnp.float32) * scale
    if len(split) > 0:
        entries = block_scale(own_key, extent, split, -0.22, 0.18) * entries
    return jnp.clip(entries, min=-bound, max=bound).astype(kind)


def setup_inputs(seed: int = 0) -> dict:
    splits = jax.random.split(jax.random.key(seed), 4)
    return {
        "chol": normal_values(splits[0], (OV, NAUX), 1.0, 6.0, ((0, 32),), jnp.float32),
        "eps_occ": jnp.clip(jax.random.uniform(splits[1], (NO,), jnp.float32, -2.0, -0.5), -2.0, -0.5),
        "eps_vir": jnp.clip(jax.random.uniform(splits[2], (NV,), jnp.float32, 0.3, 3.0), 0.3, 3.0),
    }


def reference(chol, eps_occ, eps_vir):
    total = NV * NO
    pair = (eps_vir[:, None] - eps_occ[None, :]).reshape(total)
    height = 8
    blocks = NV // height
    block_rows = height * NO
    work = jnp.zeros_like(chol)
    energies = []
    for step in range(ITERS):
        factor = chol + work

        def one_block(index):
            rows = lax.dynamic_slice_in_dim(factor, index * block_rows, block_rows, 0)
            row_pair = lax.dynamic_slice_in_dim(pair, index * block_rows, block_rows, 0)
            product = lax.dot_general(rows, factor, (((1,), (1,)), ((), ())), precision=lax.Precision.HIGHEST, preferred_element_type=jnp.float32)
            direct = product.reshape(height, NO, NV, NO)
            numerator = 2.0 * direct - jnp.transpose(direct, (0, 3, 2, 1))
            denominator = row_pair.reshape(height, NO, 1, 1) + pair.reshape(1, 1, NV, NO)
            tile = (-numerator / (jnp.float32(total) * denominator)).reshape(block_rows, total)
            return jnp.dot(tile, chol, precision=lax.Precision.HIGHEST, preferred_element_type=jnp.float32)

        work = lax.map(one_block, jnp.arange(blocks, dtype=jnp.int32)).reshape(total, NAUX)
        energies.append(jnp.sum(chol * work))
    return work, jnp.stack(energies) / jnp.float32(total)
```

```python
import functools

import jax
import jax.numpy as jnp
from jax import lax
from jax.experimental import pallas as pl
from jax.experimental.pallas import tpu as pltpu
from jax.sharding import PartitionSpec as P

ITERS = 2
LANES = 128
NT = (((1,), (1,)), ((), ()))


def split(x):
    high = x.astype(jnp.bfloat16)
    low = (x - high.astype(jnp.float32)).astype(jnp.bfloat16)
    return high, low


def flat(ref, index):
    pieces = [ref[part, index] for part in range(ref.shape[0])]
    return pieces[0] if len(pieces) == 1 else jnp.concatenate(pieces, axis=0)


def kernel(steps, rows_ref, cols_ref, chol_ref, rpair_ref, cpair_ref, out_ref, rows, cols, chol, direct, high_tile, low_tile):
    step = pl.program_id(0)
    parts, occupied, shard_virtuals, width = rows_ref.shape
    height = parts * shard_virtuals
    block = occupied // steps
    breadth = cols_ref.shape[0] * cols_ref.shape[2]
    span = block * breadth
    group = LANES // breadth

    @pl.when(step == 0)
    def _():
        def one(index, carry):
            high, low = split(flat(rows_ref, index))
            at = pl.ds(pl.multiple_of(index * height, height), height)
            rows[at, :width] = high
            rows[at, width:] = low
            return carry

        lax.fori_loop(0, occupied, one, 0)

    @pl.when(step < steps)
    def _():
        for index in range(block):
            high, low = split(flat(cols_ref, index))
            cols[index * breadth : (index + 1) * breadth, :width] = low
            cols[index * breadth : (index + 1) * breadth, width:] = high
            high, low = split(flat(chol_ref, index))
            at = pl.ds(pl.multiple_of(step * span + index * breadth, breadth), breadth)
            chol[at, :width] = high
            chol[at, width:] = low

        def one(index, carry):
            at = pl.ds(pl.multiple_of(index * block * height, block * height), block * height)
            value = lax.dot_general(rows[at, :], cols[...], NT, preferred_element_type=jnp.float32)
            value += lax.dot_general(rows[at, :width], cols[:, width:], NT, preferred_element_type=jnp.float32)
            direct[at, pl.ds(pl.multiple_of(step * span, span), span)] = value
            return carry

        lax.fori_loop(0, steps, one, 0)

    @pl.when(step >= steps)
    def _():
        first = (step - steps) * block
        lane = lax.broadcasted_iota(jnp.int32, (height, LANES), 1) // breadth

        def one(index, carry):
            lead = first + index * group
            columns = pl.ds(pl.multiple_of(lead * breadth, LANES), LANES)
            bottoms = [rpair_ref[lead + own] for own in range(group)]
            for other in range(occupied // group):
                swapped = [direct[pl.ds((other * group + m) * height, height), columns] for m in range(group)]
                to = slice(other * LANES, (other + 1) * LANES)
                tops = cpair_ref[other : other + 1, :]
                for own in range(group):
                    exchange = swapped[0] if own == 0 else pltpu.roll(swapped[0], (LANES - own * breadth) % LANES, 1)
                    for m in range(1, group):
                        shift = ((m - own) * breadth) % LANES
                        moved = pltpu.roll(swapped[m], shift, 1) if shift else swapped[m]
                        exchange = jnp.where(lane == m, moved, exchange)
                    at = pl.ds(pl.multiple_of((lead + own) * height, height), height)
                    value = (exchange - 2.0 * direct[at, to]) / (bottoms[own] + tops)
                    high, low = split(value)
                    put = pl.ds(pl.multiple_of((index * group + own) * height, height), height)
                    high_tile[put, to] = high
                    low_tile[put, to] = low
            return carry

        lax.fori_loop(0, block // group, one, 0)
        both = jnp.dot(high_tile[...], chol[...], preferred_element_type=jnp.float32)
        value = both[:, :width] + both[:, width:]
        value += jnp.dot(low_tile[...], chol[:, :width], preferred_element_type=jnp.float32)
        value = value.reshape(block, parts, shard_virtuals, width)
        for part in range(parts):
            out_ref[part] = value[:, part]


def update(rows, cols, chol, rpair, cpair):
    parts, occupied, shard_virtuals, width = rows.shape
    height = parts * shard_virtuals
    breadth = cols.shape[0] * cols.shape[2]
    steps = 6
    block = occupied // steps
    pair_columns = occupied * breadth
    column_block = (cols.shape[0], block, cols.shape[2], width)

    def of_columns(step):
        return (0, jnp.minimum(step, steps - 1), 0, 0)

    return pl.pallas_call(
        functools.partial(kernel, steps),
        grid=(2 * steps,),
        out_shape=jax.ShapeDtypeStruct(rows.shape, jnp.float32),
        in_specs=[
            pl.BlockSpec(rows.shape, lambda step: (0, 0, 0, 0)),
            pl.BlockSpec(column_block, of_columns),
            pl.BlockSpec(column_block, of_columns),
            pl.BlockSpec(rpair.shape, lambda step: (0, 0, 0)),
            pl.BlockSpec(cpair.shape, lambda step: (0, 0)),
        ],
        out_specs=pl.BlockSpec((parts, block, shard_virtuals, width), lambda step: (0, jnp.maximum(step - steps, 0), 0, 0)),
        scratch_shapes=[
            pltpu.VMEM((occupied * height, 2 * width), jnp.bfloat16),
            pltpu.VMEM((block * breadth, 2 * width), jnp.bfloat16),
            pltpu.VMEM((pair_columns, 2 * width), jnp.bfloat16),
            pltpu.VMEM((occupied * height, pair_columns), jnp.float32),
            pltpu.VMEM((block * height, pair_columns), jnp.bfloat16),
            pltpu.VMEM((block * height, pair_columns), jnp.bfloat16),
        ],
        compiler_params=pltpu.CompilerParams(
            dimension_semantics=("arbitrary",), vmem_limit_bytes=66 * 1000 * 1000
        ),
        cost_estimate=pl.CostEstimate(
            flops=12 * occupied * height * pair_columns * width, bytes_accessed=4 * width * (2 * occupied * height + 2 * pair_columns), transcendentals=0
        ),
    )(rows, cols, chol, rpair, cpair)


def gather(x, axis):
    parts = lax.all_gather(x, axis, axis=0)
    if x.shape[1] % 8:
        parts = jnp.transpose(parts, (1, 0, 2, 3)).reshape(1, x.shape[0], -1, x.shape[2])
    return parts


def shards(chol, eps_occ, eps_vir):
    n_row = lax.axis_size("row")
    n_col = lax.axis_size("col")
    row_index = lax.axis_index("row")
    col_index = lax.axis_index("col")
    shard, width = chol.shape
    occupied = eps_occ.shape[0]
    virtual = eps_vir.shape[0]
    shard_virtuals = shard // occupied
    block_virtuals = n_col * shard_virtuals
    total = virtual * occupied
    scale = jnp.float32(total)
    row_vir = lax.dynamic_slice_in_dim(eps_vir, row_index * block_virtuals, block_virtuals, 0)
    col_vir = lax.dynamic_slice_in_dim(
        eps_vir.reshape(n_row, block_virtuals), col_index * shard_virtuals, shard_virtuals, 1
    ).reshape(n_row * shard_virtuals)
    rpair = scale * (row_vir[None, :] - eps_occ[:, None])
    rpair = jnp.broadcast_to(rpair[:, :, None], (occupied, block_virtuals, LANES))
    cpair = (scale * (col_vir[None, :] - eps_occ[:, None])).reshape(-1, LANES)
    chol_t = jnp.transpose(chol.reshape(shard_virtuals, occupied, width), (1, 0, 2))
    chol_cols = gather(chol_t, "row")
    factor = chol_t
    sums = []
    for step in range(ITERS):
        rows = gather(factor, "col")
        cols = chol_cols if step == 0 else gather(factor, "row")
        partial_value = update(rows, cols, chol_cols, rpair, cpair)
        if shard_virtuals % 8:
            partial_value = jnp.transpose(
                partial_value.reshape(occupied, n_col, shard_virtuals, width), (1, 0, 2, 3)
            )
        work = lax.psum_scatter(partial_value, "col", scatter_dimension=0, tiled=False)
        factor = chol_t + work
        sums.append(jnp.sum(chol_t * work))
    energies = lax.psum(jnp.stack(sums), ("row", "col"))
    return jnp.transpose(work, (1, 0, 2)).reshape(shard, width), energies / scale


def solution(mesh):
    placed = (P(("row", "col"), None), P(), P())
    return jax.shard_map(
        shards,
        mesh=mesh,
        in_specs=placed,
        out_specs=(P(("row", "col"), None), P()),
        check_vma=False,
    )
```

```python
import functools

import jax
import jax.numpy as jnp
from jax import lax
from jax.experimental import pallas as pl
from jax.experimental.pallas import tpu as pltpu
from jax.sharding import PartitionSpec as P

ITERS = 2
LANES = 128
NT = (((1,), (1,)), ((), ()))


def split(x):
    high = x.astype(jnp.bfloat16)
    low = (x - high.astype(jnp.float32)).astype(jnp.bfloat16)
    return high, low


def flat(ref, index, turn=None):
    parts = range(ref.shape[0])
    pieces = [ref[part if turn is None else (part + turn) % len(parts), index] for part in parts]
    return pieces[0] if len(pieces) == 1 else jnp.concatenate(pieces, axis=0)


def kernel(steps, turn_ref, rows_ref, cols_ref, chol_ref, rpair_ref, cpair_ref, out_ref, rows, cols, chol, direct, high_tile, low_tile):
    step = pl.program_id(0)
    parts, occupied, shard_virtuals, width = rows_ref.shape
    height = parts * shard_virtuals
    block = occupied // steps
    breadth = cols_ref.shape[0] * cols_ref.shape[2]
    span = block * breadth
    group = LANES // breadth

    @pl.when(step == 0)
    def _():
        def one(index, carry):
            high, low = split(flat(rows_ref, index, turn_ref[0]))
            at = pl.ds(pl.multiple_of(index * height, height), height)
            rows[at, :width] = high
            rows[at, width:] = low
            return carry

        lax.fori_loop(0, occupied, one, 0)

    @pl.when(step < steps)
    def _():
        for index in range(block):
            high, low = split(flat(cols_ref, index))
            cols[index * breadth : (index + 1) * breadth, :width] = low
            cols[index * breadth : (index + 1) * breadth, width:] = high
            high, low = split(flat(chol_ref, index))
            at = pl.ds(pl.multiple_of(step * span + index * breadth, breadth), breadth)
            chol[at, :width] = high
            chol[at, width:] = low

        def one(index, carry):
            at = pl.ds(pl.multiple_of(index * block * height, block * height), block * height)
            value = lax.dot_general(rows[at, :], cols[...], NT, preferred_element_type=jnp.float32)
            value += lax.dot_general(rows[at, :width], cols[:, width:], NT, preferred_element_type=jnp.float32)
            direct[at, pl.ds(pl.multiple_of(step * span, span), span)] = value
            return carry

        lax.fori_loop(0, steps, one, 0)

    @pl.when(step >= steps)
    def _():
        first = (step - steps) * block
        lane = lax.broadcasted_iota(jnp.int32, (height, LANES), 1) // breadth

        def one(index, carry):
            lead = first + index * group
            columns = pl.ds(pl.multiple_of(lead * breadth, LANES), LANES)
            bottoms = [rpair_ref[lead + own] for own in range(group)]
            for other in range(occupied // group):
                swapped = [direct[pl.ds((other * group + m) * height, height), columns] for m in range(group)]
                to = slice(other * LANES, (other + 1) * LANES)
                tops = cpair_ref[other : other + 1, :]
                for own in range(group):
                    exchange = swapped[0] if own == 0 else pltpu.roll(swapped[0], (LANES - own * breadth) % LANES, 1)
                    for m in range(1, group):
                        shift = ((m - own) * breadth) % LANES
                        moved = pltpu.roll(swapped[m], shift, 1) if shift else swapped[m]
                        exchange = jnp.where(lane == m, moved, exchange)
                    at = pl.ds(pl.multiple_of((lead + own) * height, height), height)
                    value = (exchange - 2.0 * direct[at, to]) / (bottoms[own] + tops)
                    high, low = split(value)
                    put = pl.ds(pl.multiple_of((index * group + own) * height, height), height)
                    high_tile[put, to] = high
                    low_tile[put, to] = low
            return carry

        lax.fori_loop(0, block // group, one, 0)
        both = jnp.dot(high_tile[...], chol[...], preferred_element_type=jnp.float32)
        value = both[:, :width] + both[:, width:]
        value += jnp.dot(low_tile[...], chol[:, :width], preferred_element_type=jnp.float32)
        value = value.reshape(block, parts, shard_virtuals, width)
        for part in range(parts):
            out_ref[part] = value[:, part]


def update(turn, rows, cols, chol, rpair, cpair):
    parts, occupied, shard_virtuals, width = rows.shape
    height = parts * shard_virtuals
    breadth = cols.shape[0] * cols.shape[2]
    steps = 6
    block = occupied // steps
    pair_columns = occupied * breadth
    column_block = (cols.shape[0], block, cols.shape[2], width)

    def of_columns(step):
        return (0, jnp.minimum(step, steps - 1), 0, 0)

    return pl.pallas_call(
        functools.partial(kernel, steps),
        grid=(2 * steps,),
        out_shape=jax.ShapeDtypeStruct(rows.shape, jnp.float32),
        in_specs=[
            pl.BlockSpec(memory_space=pltpu.SMEM),
            pl.BlockSpec(rows.shape, lambda step: (0, 0, 0, 0)),
            pl.BlockSpec(column_block, of_columns),
            pl.BlockSpec(column_block, of_columns),
            pl.BlockSpec(rpair.shape, lambda step: (0, 0, 0)),
            pl.BlockSpec(cpair.shape, lambda step: (0, 0)),
        ],
        out_specs=pl.BlockSpec((parts, block, shard_virtuals, width), lambda step: (0, jnp.maximum(step - steps, 0), 0, 0)),
        scratch_shapes=[
            pltpu.VMEM((occupied * height, 2 * width), jnp.bfloat16),
            pltpu.VMEM((block * breadth, 2 * width), jnp.bfloat16),
            pltpu.VMEM((pair_columns, 2 * width), jnp.bfloat16),
            pltpu.VMEM((occupied * height, pair_columns), jnp.float32),
            pltpu.VMEM((block * height, pair_columns), jnp.bfloat16),
            pltpu.VMEM((block * height, pair_columns), jnp.bfloat16),
        ],
        compiler_params=pltpu.CompilerParams(
            dimension_semantics=("arbitrary",), vmem_limit_bytes=66 * 1000 * 1000
        ),
        cost_estimate=pl.CostEstimate(
            flops=12 * occupied * height * pair_columns * width, bytes_accessed=4 * width * (2 * occupied * height + 2 * pair_columns), transcendentals=0
        ),
    )(turn, rows, cols, chol, rpair, cpair)


def gather(x, axis):
    parts = lax.all_gather(x, axis, axis=0)
    if x.shape[1] % 8:
        parts = jnp.transpose(parts, (1, 0, 2, 3)).reshape(1, x.shape[0], -1, x.shape[2])
    return parts


def passed(x, axis):
    n = lax.axis_size(axis)
    blocks = [x]
    for k in range(1, n):
        blocks.append(lax.ppermute(x, axis, [(j, (j - k) % n) for j in range(n)]))
    return jnp.stack(blocks)


def shards(chol, eps_occ, eps_vir):
    n_row = lax.axis_size("row")
    n_col = lax.axis_size("col")
    row_index = lax.axis_index("row")
    col_index = lax.axis_index("col")
    shard, width = chol.shape
    occupied = eps_occ.shape[0]
    virtual = eps_vir.shape[0]
    shard_virtuals = shard // occupied
    block_virtuals = n_col * shard_virtuals
    total = virtual * occupied
    scale = jnp.float32(total)
    row_vir = lax.dynamic_slice_in_dim(eps_vir, row_index * block_virtuals, block_virtuals, 0)
    col_vir = lax.dynamic_slice_in_dim(
        eps_vir.reshape(n_row, block_virtuals), col_index * shard_virtuals, shard_virtuals, 1
    ).reshape(n_row * shard_virtuals)
    rpair = scale * (row_vir[None, :] - eps_occ[:, None])
    rpair = jnp.broadcast_to(rpair[:, :, None], (occupied, block_virtuals, LANES))
    cpair = (scale * (col_vir[None, :] - eps_occ[:, None])).reshape(-1, LANES)
    chol_t = jnp.transpose(chol.reshape(shard_virtuals, occupied, width), (1, 0, 2))
    chol_cols = gather(chol_t, "row")
    factor = chol_t
    sums = []
    for step in range(ITERS):
        if shard_virtuals % 8:
            rows = gather(factor, "col")
            turn = jnp.zeros((1,), jnp.int32)
        else:
            rows = passed(factor, "col")
            turn = jnp.full((1,), n_col - col_index, jnp.int32)
        cols = chol_cols if step == 0 else gather(factor, "row")
        partial_value = update(turn, rows, cols, chol_cols, rpair, cpair)
        if shard_virtuals % 8:
            partial_value = jnp.transpose(
                partial_value.reshape(occupied, n_col, shard_virtuals, width), (1, 0, 2, 3)
            )
        work = lax.psum_scatter(partial_value, "col", scatter_dimension=0, tiled=False)
        factor = chol_t + work
        sums.append(jnp.sum(chol_t * work))
    energies = lax.psum(jnp.stack(sums), ("row", "col"))
    return jnp.transpose(work, (1, 0, 2)).reshape(shard, width), energies / scale


def solution(mesh):
    placed = (P(("row", "col"), None), P(), P())
    return jax.shard_map(
        shards,
        mesh=mesh,
        in_specs=placed,
        out_specs=(P(("row", "col"), None), P()),
        check_vma=False,
    )
```
